256 devices in a mesh: feat: 64 (over z_lo, y, x), tgt: 4 (over z_hi, core).
Axes of the slice: x: 4, y: 4, z: 8 (z_hi: 2, z_lo: 4; z = z_hi * 4 + z_lo), core: 2. Of those that a mesh axis runs over, the one named last changes fastest.
Arguments:
- tokens: bfloat16 [192, 4096], P('feat'), may hold values from -6 to 6
- encoder_weight: bfloat16 [4096, 16384], P(None, 'feat'), may hold values from -0.09375 to 0.09375
- encoder_bias: float32 [16384], P('feat'), may hold values from -1 to 0.25
- decoder_weight: bfloat16 [4, 16384, 4096], P('tgt', 'feat'), may hold values from -0.046875 to 0.046875
- decoder_bias: float32 [4, 4096], P('tgt'), may hold values from -3 to 3
- targets: bfloat16 [4, 192, 4096], P('tgt', 'feat'), may hold values from -6 to 6
Outputs:
- encoder_grad: float32 [4096, 16384], P(None, ('feat', 'tgt'))
- encoder_bias_grad: float32 [16384], P(('feat', 'tgt'))
- decoder_grad: float32 [4, 16384, 4096], P('tgt', 'feat')
- decoder_bias_grad: float32 [4, 4096], P('tgt')
The draws below stay inside these ranges and needn't reach their ends.
All inputs are finite; a program needn't handle non-finite values.
Results may differ from the reference program's by a relative error of at most 0.005.
Values may be sent and summed in bfloat16 or wider, within the bound.
No kernel may reach another device: no remote copies, remote signals or barrier semaphores. Data moves between devices by JAX's collectives and lax.ppermute only.
A program may use at most 64 MiB of HBM per device.

```python
import jax
import jax.numpy as jnp

D = 4096
F = 16384
LAYERS = 4
TOKENS = 192


def block_levels(key, dims, cuts, least, top_value):
    factor_of, own = 1.0, jax.random.fold_in(key, 6)
    for axis_at, blocks in cuts:
        heights = jnp.exp(jax.random.uniform(jax.random.fold_in(own, axis_at), (blocks,), jnp.float32, least / len(cuts), top_value / len(cuts)))
        factor_of = factor_of * jnp.repeat(heights, dims[axis_at] // blocks).reshape([-1 if axis == axis_at else 1 for axis in range(len(dims))])
    return factor_of


def noise(key, extent, deviation, bound, cuts=(), dtype=jnp.bfloat16):
    factor_of = block_levels(key, extent, cuts, -0.22, 0.18) if cuts else 1.0
    drawn = jax.random.normal(key, extent, jnp.float32) * deviation * factor_of
    return jnp.minimum(jnp.maximum(drawn, -bound), bound).astype(dtype)


def setup_inputs(seed: int = 0) -> dict:
    keys = jax.random.split(jax.random.key(seed), 7)
    return {
        "tokens": noise(keys[0], (TOKENS, D), 1.0, 6.0, ((0, 64),)),
        "encoder_weight": noise(keys[1], (D, F), D ** -0.5, 0.09375, ((1, 64),)),
        "encoder_bias": jnp.clip(-1.0 + 1.25 * jax.random.uniform(keys[2], (F,), jnp.float32) ** block_levels(keys[2], (F,), ((0, 64),), -0.2, 0.2), -1.0, 0.25),
        "decoder_weight": noise(keys[3], (LAYERS, F, D), F ** -0.5, 0.046875, ((0, 4), (1, 64))),
        "decoder_bias": noise(keys[4], (LAYERS, D), 0.5, 3.0, ((0, 4),), jnp.float32),
        "targets": noise(keys[5], (LAYERS, TOKENS, D), 1.0, 6.0, ((0, 4), (1, 64))),
    }


def reference(tokens, encoder_weight, encoder_bias, decoder_weight, decoder_bias, targets):
    pre_act = jnp.dot(tokens, encoder_weight, preferred_element_type=jnp.float32) + encoder_bias
    feats = (jnp.maximum(pre_act, 0.0) ** 2).astype(jnp.bfloat16)
    back_grad = jnp.zeros(pre_act.shape, jnp.float32)
    decoder_grads = []
    bias_grads = []
    for target_index in range(LAYERS):
        pred = jnp.dot(feats, decoder_weight[target_index], preferred_element_type=jnp.float32) + decoder_bias[target_index]
        recon_error = (pred - targets[target_index].astype(jnp.float32)).astype(jnp.bfloat16)
        decoder_grads.append(jnp.dot(feats.T, recon_error, preferred_element_type=jnp.float32))
        bias_grads.append(jnp.sum(recon_error.astype(jnp.float32), axis=0))
        back_grad = back_grad + jnp.dot(recon_error, decoder_weight[target_index].T, preferred_element_type=jnp.float32)
    act_grad = back_grad * (2.0 * jnp.maximum(pre_act, 0.0))
    encoder_bias_grad = jnp.sum(act_grad, axis=0)
    pre_grad = act_grad.astype(jnp.bfloat16)
    encoder_grad = jnp.dot(tokens.T, pre_grad, preferred_element_type=jnp.float32)
    return encoder_grad, encoder_bias_grad, jnp.stack(decoder_grads), jnp.stack(bias_grads)
```

```python
import jax
import jax.numpy as jnp
from jax import lax
from jax.sharding import Mesh, PartitionSpec as P

BF16 = jnp.bfloat16
F32 = jnp.float32
FEAT = ("zl", "y", "x")
TGT = ("zh", "core")
SWAP = [(0, 1), (1, 0)]


def spread(block, axes, count):
    copies = jnp.broadcast_to(block[None], (count,) + block.shape)
    return lax.all_to_all(copies, axes, 0, 0, tiled=True)


def gather_tokens(tokens):
    members = lax.axis_size(FEAT)
    mine, width = tokens.shape
    half = width // 2
    core = lax.axis_index("core")
    part = lax.dynamic_slice_in_dim(tokens, core * half, half, 1)
    flat = part.reshape(mine * half // 128, 128)
    own = spread(flat, FEAT, members)
    other = lax.ppermute(own, "core", SWAP)
    low = jnp.where(core == 0, own, other).reshape(members * mine, half)
    high = jnp.where(core == 0, other, own).reshape(members * mine, half)
    return jnp.concatenate([low, high], axis=1)


def body(tokens, encoder_weight, encoder_bias, decoder_weight, decoder_bias, targets):
    plane = lax.axis_size(("y", "x"))
    depth = lax.axis_size("zl")
    all_rows = gather_tokens(tokens)
    count, width = all_rows.shape
    chunk = width // plane
    pre_act = jnp.dot(all_rows, encoder_weight, preferred_element_type=F32) + encoder_bias
    positive = jnp.maximum(pre_act, 0.0)
    feats = (positive**2).astype(BF16)
    weight = decoder_weight[0]
    target = targets[0].astype(F32)

    partial = jnp.dot(feats, weight, preferred_element_type=F32)
    rows = lax.broadcasted_iota(jnp.int32, (count, 1), 0)
    first = lax.axis_index(FEAT) * target.shape[0]
    for i in range(target.shape[0]):
        partial = partial - jnp.where(rows == first + i, target[i : i + 1], 0.0)
    pieces = partial.astype(BF16).reshape(count, plane, chunk).transpose(1, 0, 2)
    pieces = lax.all_to_all(pieces, ("y", "x"), 0, 0, tiled=True)
    mine = jnp.sum(pieces.astype(F32), axis=0).astype(BF16)
    peers = [
        lax.ppermute(mine, "zl", [(i, i ^ k) for i in range(depth)]) for k in range(1, depth)
    ]
    a, b, c, d = [v.astype(F32) for v in [mine] + peers]
    offset = lax.axis_index(("y", "x")) * chunk
    bias = lax.dynamic_slice_in_dim(decoder_bias[0], offset, chunk, 0)
    error_part = (((a + b) + (c + d)) + bias).astype(BF16)
    recon_error = spread(error_part, ("y", "x"), plane).transpose(1, 0, 2).reshape(count, width)

    back_grad = lax.dot_general(
        weight, recon_error, (((1,), (1,)), ((), ())), preferred_element_type=F32
    )
    quarter = back_grad.shape[0] // 4
    quarters = back_grad.reshape(2, 2, quarter, count)
    zh, core = lax.axis_index("zh"), lax.axis_index("core")
    keep = lax.dynamic_index_in_dim(quarters, zh, 0, False)
    send = lax.dynamic_index_in_dim(quarters, 1 - zh, 0, False)
    pair = keep + lax.ppermute(send, "zh", SWAP)
    keep = lax.dynamic_index_in_dim(pair, core, 0, False)
    send = lax.dynamic_index_in_dim(pair, 1 - core, 0, False)
    share = (keep + lax.ppermute(send, "core", SWAP)).T

    decoder_grad = lax.dot_general(
        feats, recon_error, (((0,), (0,)), ((), ())), preferred_element_type=F32
    )
    bias_grad = jnp.sum(recon_error.astype(F32), axis=0)
    offset = lax.axis_index(TGT) * quarter
    act_grad = share * (2.0 * lax.dynamic_slice_in_dim(positive, offset, quarter, 1))
    encoder_bias_grad = jnp.sum(act_grad, axis=0)
    pre_grad = act_grad.astype(BF16)
    encoder_grad = lax.dot_general(
        all_rows, pre_grad, (((0,), (0,)), ((), ())), preferred_element_type=F32
    )
    return encoder_grad, encoder_bias_grad, decoder_grad[None], bias_grad[None]


def solution(mesh):
    split = Mesh(mesh.devices.reshape(4, 4, 4, 2, 2), FEAT + TGT)
    return jax.shard_map(
        body,
        mesh=split,
        in_specs=(
            P(FEAT, None),
            P(None, FEAT),
            P(FEAT),
            P(TGT, FEAT, None),
            P(TGT, None),
            P(TGT, FEAT, None),
        ),
        out_specs=(
            P(None, FEAT + TGT),
            P(FEAT + TGT),
            P(TGT, FEAT, None),
            P(TGT, None),
        ),
        check_vma=False,
    )
```

```python
import functools

import jax
import jax.numpy as jnp
from jax import lax
from jax.experimental import pallas as pl
from jax.experimental.pallas import tpu as pltpu
from jax.sharding import Mesh, PartitionSpec as P

BF16 = jnp.bfloat16
F32 = jnp.float32
FEAT = ("zl", "y", "x")
TGT = ("zh", "core")
PLANE = ("y", "x")
TN = (((0,), (0,)), ((), ()))
NT = (((1,), (1,)), ((), ()))

J, ROWS, DEPTH, D, FEATS = 16, 3, 4, 4096, 256
COUNT = J * ROWS * DEPTH
CHUNK = D // J
WIDE = D // 4


def in_vmem(x):
    return pltpu.with_memory_space_constraint(x, pltpu.VMEM)


def call(kernel, outs, *args, vmem=(), **kwargs):
    args = [in_vmem(a) if i in vmem else a for i, a in enumerate(args)]
    return pl.pallas_call(
        kernel,
        out_shape=outs,
        compiler_params=pltpu.CompilerParams(vmem_limit_bytes=40 * 1024 * 1024),
        **kwargs,
    )(*args)


def pack_kernel(own_ref, below_ref, above_ref, far_ref, out_ref):
    core, zl = lax.axis_index("core"), lax.axis_index("zl")
    sub = lax.broadcasted_iota(jnp.int32, (8, WIDE), 0)
    start = pl.multiple_of(core * (D // 2), D // 2)
    sources = [(own_ref, 0), (below_ref, 3), (above_ref, 1), (far_ref, 2)]
    blocks = [(ref[:, pl.ds(start, D // 2)].astype(F32), (zl + step) % 4) for ref, step in sources]
    for i in range(ROWS):
        tile = jnp.zeros((8, WIDE), F32)
        for block, depth in blocks:
            for h in range(2):
                row = block[i : i + 1, h * WIDE : (h + 1) * WIDE]
                tile = jnp.where(sub == depth + 4 * h, row, tile)
        tile = tile.astype(BF16)
        for j in range(J):
            out_ref[j, i] = tile


def forward_kernel(own_ref, other_ref, enc_ref, enc_bias_ref, dec_ref, target_ref, out_ref, pos_ref, feats_ref, acc_ref):
    core, zl = lax.axis_index("core"), lax.axis_index("zl")
    member = lax.axis_index(PLANE)
    sums = []
    for h in range(2):
        mine = pl.multiple_of(core * (D // 2) + h * WIDE, WIDE)
        theirs = pl.multiple_of((1 - core) * (D // 2) + h * WIDE, WIDE)
        sums.append(
            jnp.dot(own_ref[...], enc_ref[pl.ds(mine, WIDE), :], preferred_element_type=F32)
            + jnp.dot(other_ref[...], enc_ref[pl.ds(theirs, WIDE), :], preferred_element_type=F32)
        )
    low, high = [s.reshape(COUNT // 8, 2, 8, FEATS) for s in sums]
    sub = lax.broadcasted_iota(jnp.int32, (COUNT // 8, 8, FEATS), 1)
    both = []
    for g in range(2):
        part = jnp.where(sub < 4, low[:, g], high[:, g])
        both.append(part + pltpu.roll(part, 4, 1))
    pre = jnp.where(sub < 4, both[0], both[1]).reshape(COUNT, FEATS) + enc_bias_ref[...]
    positive = jnp.maximum(pre, 0.0)
    pos_ref[...] = positive
    feats = (positive * positive).astype(BF16)
    feats_ref[...] = feats
    lane_sub = lax.broadcasted_iota(jnp.int32, (8, CHUNK), 0)
    for j in range(J):
        acc_ref[j % 2] = jnp.dot(feats, dec_ref[:, j * CHUNK : (j + 1) * CHUNK], preferred_element_type=F32)
        for i in range(ROWS):
            group = ROWS * member + i
            tile = pl.ds(pl.multiple_of(8 * (group // 2), 8), 8)
            row = 4 * (group % 2) + zl
            value = target_ref[i : i + 1, j * CHUNK : (j + 1) * CHUNK].astype(F32)
            acc_ref[j % 2, tile, :] = acc_ref[j % 2, tile, :] - jnp.where(lane_sub == row, value, 0.0)
        out_ref[j] = acc_ref[j % 2].astype(BF16)


def sum_kernel(pieces_ref, out_ref):
    total = pieces_ref[0].astype(F32)
    for j in range(1, J):
        total = total + pieces_ref[j].astype(F32)
    out_ref[...] = total.astype(BF16)


def error_kernel(a_ref, b_ref, c_ref, d_ref, bias_ref, out_ref):
    member = lax.axis_index(PLANE)
    a, b, c, d = [ref[...].astype(F32) for ref in (a_ref, b_ref, c_ref, d_ref)]
    bias = bias_ref[:, pl.ds(pl.multiple_of(member * CHUNK, CHUNK), CHUNK)]
    error = (((a + b) + (c + d)) + bias).astype(BF16)
    for j in range(J):
        out_ref[j] = error


def back_kernel(error_ref, dec_ref, keep_ref, send_ref):
    zh = lax.axis_index("zh")
    total = jnp.zeros((COUNT, FEATS), F32)
    for j in range(J):
        total = total + lax.dot_general(
            error_ref[j], dec_ref[:, j * CHUNK : (j + 1) * CHUNK], NT, preferred_element_type=F32
        )
    half = FEATS // 2
    keep_ref[...] = jnp.where(zh == 0, total[:, :half], total[:, half:])
    send_ref[...] = jnp.where(zh == 0, total[:, half:], total[:, :half]).astype(BF16)


def decoder_kernel(error_ref, feats_ref, grad_ref, bias_ref):
    grad_ref[...] = lax.dot_general(feats_ref[...], error_ref[0], TN, preferred_element_type=F32)
    bias_ref[...] = jnp.sum(error_ref[0].astype(F32), axis=0, keepdims=True)


def encoder_kernel(own_ref, other_ref, keep_ref, near_ref, far_ref, cross_ref, pos_ref, grad_ref, bias_ref):
    core, zh = lax.axis_index("core"), lax.axis_index("zh")
    quarter = FEATS // 4
    half = pl.multiple_of(zh * (FEATS // 2), FEATS // 2)
    share = (keep_ref[...] + near_ref[...]) + (far_ref[...].astype(F32) + cross_ref[...].astype(F32))
    act = share * (2.0 * pos_ref[:, pl.ds(half, FEATS // 2)])
    act = jnp.where(core == 0, act[:, :quarter], act[:, quarter:])
    bias_ref[...] = jnp.sum(act, axis=0, keepdims=True)
    tiles = act.astype(BF16).astype(F32).reshape(COUNT // 8, 8, quarter)
    turned = pltpu.roll(tiles, 4, 1)
    sub = lax.broadcasted_iota(jnp.int32, tiles.shape, 1)
    zero = jnp.zeros_like(tiles)
    low = jnp.stack([jnp.where(sub < 4, tiles, zero), jnp.where(sub < 4, turned, zero)], axis=1)
    high = jnp.stack([jnp.where(sub < 4, zero, turned), jnp.where(sub < 4, zero, tiles)], axis=1)
    for h, side in enumerate((low, high)):
        side = side.reshape(2 * COUNT, quarter).astype(BF16)
        for ref, owner in ((own_ref, core), (other_ref, 1 - core)):
            start = pl.multiple_of(owner * (D // 2) + h * WIDE, WIDE)
            grad_ref[:, pl.ds(start, WIDE)] = lax.dot_general(side, ref[...], TN, preferred_element_type=F32)


def ring(step):
    index = lambda z: (z % 4) * 2 + z // 4
    return [(index(z), index((z + step) % 8)) for z in range(8)]


def mirror(axes, size, key):
    return lambda x: lax.ppermute(x, axes, [(i, i ^ key) for i in range(size)])


def body(tokens, encoder_weight, encoder_bias, decoder_weight, decoder_bias, targets):
    sds = jax.ShapeDtypeStruct
    below, above, far = [lax.ppermute(tokens, ("zl", "zh"), ring(step)) for step in (1, 7, 2)]
    packed = call(pack_kernel, pltpu.VMEM((J, ROWS, 8, WIDE), BF16), tokens, below, above, far)
    own = lax.all_to_all(packed, PLANE, 0, 0, tiled=True).reshape(2 * COUNT, WIDE)
    other = mirror("core", 2, 1)(own)
    dec = decoder_weight[0]
    pieces, positive, feats = call(
        forward_kernel,
        (pltpu.VMEM((J, COUNT, CHUNK), BF16), pltpu.VMEM((COUNT, FEATS), F32), pltpu.VMEM((COUNT, FEATS), BF16)),
        own, other, encoder_weight, encoder_bias[None], dec, targets[0],
        vmem=(0, 1, 2, 4),
        scratch_shapes=[pltpu.VMEM((2, COUNT, CHUNK), F32)],
    )
    pieces = lax.all_to_all(pieces, PLANE, 0, 0, tiled=True)
    part = call(sum_kernel, pltpu.VMEM((COUNT, CHUNK), BF16), pieces, vmem=(0,))
    peers = [mirror("zl", DEPTH, key)(part) for key in (1, 2, 3)]
    copies = call(error_kernel, pltpu.VMEM((J, COUNT, CHUNK), BF16), part, *peers, decoder_bias, vmem=(0, 1, 2, 3))
    errors = lax.all_to_all(copies, PLANE, 0, 0, tiled=True)
    keep, send = call(
        back_kernel,
        (pltpu.VMEM((COUNT, FEATS // 2), F32), pltpu.VMEM((COUNT, FEATS // 2), BF16)),
        errors, dec,
        vmem=(0, 1),
    )
    near = mirror(TGT, 4, 1)(keep)
    back = [mirror(TGT, 4, key)(send) for key in (2, 3)]
    decoder_grad, bias_grad = call(
        decoder_kernel,
        (sds((FEATS, D), F32), sds((1, D), F32)),
        errors, feats,
        vmem=(0, 1),
        grid=(J,),
        in_specs=[
            pl.BlockSpec((1, COUNT, CHUNK), lambda j: (j, 0, 0)),
            pl.BlockSpec((COUNT, FEATS), lambda j: (0, 0)),
        ],
        out_specs=(pl.BlockSpec((FEATS, CHUNK), lambda j: (0, j)), pl.BlockSpec((1, CHUNK), lambda j: (0, j))),
    )
    encoder_grad, encoder_bias_grad = call(
        encoder_kernel,
        (sds((FEATS // 4, D), F32), sds((1, FEATS // 4), F32)),
        own, other, keep, near, *back, positive,
        vmem=(0, 1, 2, 3, 4, 5, 6),
    )
    return encoder_grad.T, encoder_bias_grad[0], decoder_grad[None], bias_grad


def solution(mesh):
    split = Mesh(mesh.devices.reshape(4, 4, 4, 2, 2), FEAT + TGT)
    return jax.shard_map(
        body,
        mesh=split,
        in_specs=(
            P(FEAT, None),
            P(None, FEAT),
            P(FEAT),
            P(TGT, FEAT, None),
            P(TGT, None),
            P(TGT, FEAT, None),
        ),
        out_specs=(
            P(None, FEAT + TGT),
            P(FEAT + TGT),
            P(TGT, FEAT, None),
            P(TGT, None),
        ),
        check_vma=False,
    )
```

```python
import jax
import jax.numpy as jnp
import numpy as np
from jax import lax
from jax.experimental import pallas as pl
from jax.experimental.pallas import tpu as pltpu
from jax.sharding import Mesh, PartitionSpec as P

BF16 = jnp.bfloat16
F32 = jnp.float32
FEAT = ("zl", "y", "x")
TGT = ("zh", "core")
TN = (((0,), (0,)), ((), ()))
NT = (((1,), (1,)), ((), ()))

J, ROWS, DEPTH, D, FEATS = 16, 3, 4, 4096, 256
COUNT = J * ROWS * DEPTH
CHUNK = D // J
WIDE = D // 4
STEP = 4


def position(y, x):
    return 4 * y + x + (y % 2) * (3 - 2 * x)


def plane_groups(shape):
    ids = np.arange(np.prod(shape)).reshape(shape)
    order = sorted(np.ndindex(shape[1], shape[2]), key=lambda p: position(*p))
    return [
        [int(ids[z, y, x, zh, core]) for y, x in order]
        for z, zh, core in np.ndindex(shape[0], *shape[3:])
    ]


def exchange(x):
    return lax.all_to_all(x, FEAT + TGT, 0, 0, axis_index_groups=plane_groups((4, 4, 4, 2, 2)), tiled=True)


def in_vmem(x):
    return pltpu.with_memory_space_constraint(x, pltpu.VMEM)


def call(kernel, outs, *args, vmem=(), **kwargs):
    args = [in_vmem(a) if i in vmem else a for i, a in enumerate(args)]
    return pl.pallas_call(
        kernel,
        out_shape=outs,
        compiler_params=pltpu.CompilerParams(vmem_limit_bytes=40 * 1024 * 1024),
        **kwargs,
    )(*args)


def load_kernel(tokens_ref, enc_ref, tokens_out, enc_out, sems):
    copies = [
        pltpu.make_async_copy(tokens_ref, tokens_out, sems.at[0]),
        pltpu.make_async_copy(enc_ref, enc_out, sems.at[1]),
    ]
    for copy in copies:
        copy.start()
    for copy in copies:
        copy.wait()


def pack_kernel(own_ref, below_ref, above_ref, far_ref, out_ref):
    core, zl = lax.axis_index("core"), lax.axis_index("zl")
    sub = lax.broadcasted_iota(jnp.int32, (8, WIDE), 0)
    start = pl.multiple_of(core * (D // 2), D // 2)
    sources = [(own_ref, 0), (below_ref, 3), (above_ref, 1), (far_ref, 2)]
    blocks = [(ref[:, pl.ds(start, D // 2)].astype(F32), (zl + step) % 4) for ref, step in sources]
    for i in range(ROWS):
        tile = jnp.zeros((8, WIDE), F32)
        for block, depth in blocks:
            for h in range(2):
                row = block[i : i + 1, h * WIDE : (h + 1) * WIDE]
                tile = jnp.where(sub == depth + 4 * h, row, tile)
        tile = tile.astype(BF16)
        for j in range(J):
            out_ref[j, i] = tile


def forward_kernel(own_ref, other_ref, enc_ref, enc_bias_ref, dec_ref, target_ref, out_ref, pos_ref, feats_ref, acc_ref):
    core, zl = lax.axis_index("core"), lax.axis_index("zl")
    member = position(lax.axis_index("y"), lax.axis_index("x"))
    sums = []
    for h in range(2):
        mine = pl.multiple_of(core * (D // 2) + h * WIDE, WIDE)
        theirs = pl.multiple_of((1 - core) * (D // 2) + h * WIDE, WIDE)
        sums.append(
            jnp.dot(own_ref[...], enc_ref[pl.ds(mine, WIDE), :], preferred_element_type=F32)
            + jnp.dot(other_ref[...], enc_ref[pl.ds(theirs, WIDE), :], preferred_element_type=F32)
        )
    low, high = [s.reshape(COUNT // 8, 2, 8, FEATS) for s in sums]
    sub = lax.broadcasted_iota(jnp.int32, (COUNT // 8, 8, FEATS), 1)
    both = []
    for g in range(2):
        part = jnp.where(sub < 4, low[:, g], high[:, g])
        both.append(part + pltpu.roll(part, 4, 1))
    pre = jnp.where(sub < 4, both[0], both[1]).reshape(COUNT, FEATS) + enc_bias_ref[...]
    positive = jnp.maximum(pre, 0.0)
    pos_ref[...] = positive
    feats = (positive * positive).astype(BF16)
    feats_ref[...] = feats
    lane_sub = lax.broadcasted_iota(jnp.int32, (8, CHUNK), 0)
    for j in range(J):
        acc_ref[j % 2] = jnp.dot(feats, dec_ref[:, j * CHUNK : (j + 1) * CHUNK], preferred_element_type=F32)
        for i in range(ROWS):
            group = ROWS * member + i
            tile = pl.ds(pl.multiple_of(8 * (group // 2), 8), 8)
            row = 4 * (group % 2) + zl
            value = target_ref[i : i + 1, j * CHUNK : (j + 1) * CHUNK].astype(F32)
            acc_ref[j % 2, tile, :] = acc_ref[j % 2, tile, :] - jnp.where(lane_sub == row, value, 0.0)
        out_ref[j] = acc_ref[j % 2].astype(BF16)


def sum_kernel(pieces_ref, out_ref):
    total = pieces_ref[0].astype(F32)
    for j in range(1, J):
        total = total + pieces_ref[j].astype(F32)
    out_ref[...] = total.astype(BF16)


def error_kernel(a_ref, b_ref, c_ref, d_ref, bias_ref, out_ref):
    member = position(lax.axis_index("y"), lax.axis_index("x"))
    a, b, c, d = [ref[...].astype(F32) for ref in (a_ref, b_ref, c_ref, d_ref)]
    bias = bias_ref[:, pl.ds(pl.multiple_of(member * CHUNK, CHUNK), CHUNK)]
    error = (((a + b) + (c + d)) + bias).astype(BF16)
    for j in range(J):
        out_ref[j] = error


def back_kernel(error_ref, dec_ref, keep_ref, send_ref):
    zh = lax.axis_index("zh")
    total = jnp.zeros((COUNT, FEATS), F32)
    for j in range(J):
        total = total + lax.dot_general(
            error_ref[j], dec_ref[:, j * CHUNK : (j + 1) * CHUNK], NT, preferred_element_type=F32
        )
    half = FEATS // 2
    keep_ref[...] = jnp.where(zh == 0, total[:, :half], total[:, half:])
    send_ref[...] = jnp.where(zh == 0, total[:, half:], total[:, :half]).astype(BF16)


def decoder_kernel(error_ref, feats_ref, grad_ref, bias_ref, done_ref):
    error = jnp.concatenate([error_ref[j] for j in range(STEP)], axis=1)
    grad_ref[...] = lax.dot_general(feats_ref[...], error, TN, preferred_element_type=F32)
    bias_ref[...] = jnp.sum(error.astype(F32), axis=0, keepdims=True)
    done_ref[...] = jnp.zeros_like(done_ref)


def pair_kernel(keep_ref, peer_ref, after_ref, out_ref):
    out_ref[...] = keep_ref[...] + peer_ref[...].astype(F32)


def encoder_kernel(own_ref, other_ref, pair_ref, near_ref, pos_ref, grad_ref, bias_ref):
    core, zh = lax.axis_index("core"), lax.axis_index("zh")
    quarter = FEATS // 4
    half = pl.multiple_of(zh * (FEATS // 2), FEATS // 2)
    share = pair_ref[...] + near_ref[...]
    act = share * (2.0 * pos_ref[:, pl.ds(half, FEATS // 2)])
    act = jnp.where(core == 0, act[:, :quarter], act[:, quarter:])
    bias_ref[...] = jnp.sum(act, axis=0, keepdims=True)
    tiles = act.astype(BF16).astype(F32).reshape(COUNT // 8, 8, quarter)
    turned = pltpu.roll(tiles, 4, 1)
    sub = lax.broadcasted_iota(jnp.int32, tiles.shape, 1)
    zero = jnp.zeros_like(tiles)
    low = jnp.stack([jnp.where(sub < 4, tiles, zero), jnp.where(sub < 4, turned, zero)], axis=1)
    high = jnp.stack([jnp.where(sub < 4, zero, turned), jnp.where(sub < 4, zero, tiles)], axis=1)
    for h, side in enumerate((low, high)):
        side = side.reshape(2 * COUNT, quarter).astype(BF16)
        for ref, owner in ((own_ref, core), (other_ref, 1 - core)):
            start = pl.multiple_of(owner * (D // 2) + h * WIDE, WIDE)
            grad_ref[:, pl.ds(start, WIDE)] = lax.dot_general(side, ref[...], TN, preferred_element_type=F32)


def ring(step):
    index = lambda z: (z % 4) * 2 + z // 4
    return [(index(z), index((z + step) % 8)) for z in range(8)]


def mirror(axes, size, key):
    return lambda x: lax.ppermute(x, axes, [(i, i ^ key) for i in range(size)])


def body(tokens, encoder_weight, encoder_bias, decoder_weight, decoder_bias, targets):
    sds = jax.ShapeDtypeStruct
    below, above, far = [lax.ppermute(tokens, ("zl", "zh"), ring(step)) for step in (1, 7, 2)]
    tokens, encoder_weight = call(
        load_kernel,
        (pltpu.VMEM(tokens.shape, BF16), pltpu.VMEM(encoder_weight.shape, BF16)),
        tokens, encoder_weight,
        in_specs=[pl.BlockSpec(memory_space=pl.ANY)] * 2,
        scratch_shapes=[pltpu.SemaphoreType.DMA((2,))],
    )
    packed = call(pack_kernel, pltpu.VMEM((J, ROWS, 8, WIDE), BF16), tokens, below, above, far)
    own = exchange(packed).reshape(2 * COUNT, WIDE)
    other = mirror("core", 2, 1)(own)
    dec = decoder_weight[0]
    pieces, positive, feats = call(
        forward_kernel,
        (pltpu.VMEM((J, COUNT, CHUNK), BF16), pltpu.VMEM((COUNT, FEATS), F32), pltpu.VMEM((COUNT, FEATS), BF16)),
        own, other, encoder_weight, encoder_bias[None], dec, targets[0],
        vmem=(0, 1, 2, 4),
        scratch_shapes=[pltpu.VMEM((2, COUNT, CHUNK), F32)],
    )
    pieces = exchange(pieces)
    part = call(sum_kernel, pltpu.VMEM((COUNT, CHUNK), BF16), pieces, vmem=(0,))
    peers = [mirror("zl", DEPTH, key)(part) for key in (1, 2, 3)]
    copies = call(error_kernel, pltpu.VMEM((J, COUNT, CHUNK), BF16), part, *peers, decoder_bias, vmem=(0, 1, 2, 3))
    errors = exchange(copies)
    keep, send = call(
        back_kernel,
        (pltpu.VMEM((COUNT, FEATS // 2), F32), pltpu.VMEM((COUNT, FEATS // 2), BF16)),
        errors, dec,
        vmem=(0, 1),
    )
    peer = mirror("zh", 2, 1)(send)
    decoder_grad, bias_grad, done = call(
        decoder_kernel,
        (sds((FEATS, D), F32), sds((1, D), F32), pltpu.VMEM((8, 128), F32)),
        errors, feats,
        vmem=(0, 1),
        grid=(J // STEP,),
        in_specs=[
            pl.BlockSpec((STEP, COUNT, CHUNK), lambda j: (j, 0, 0)),
            pl.BlockSpec((COUNT, FEATS), lambda j: (0, 0)),
        ],
        out_specs=(
            pl.BlockSpec((FEATS, STEP * CHUNK), lambda j: (0, j)),
            pl.BlockSpec((1, STEP * CHUNK), lambda j: (0, j)),
            pl.BlockSpec((8, 128), lambda j: (0, 0)),
        ),
    )
    pair = call(pair_kernel, pltpu.VMEM((COUNT, FEATS // 2), F32), keep, peer, done, vmem=(0, 1, 2))
    near = mirror("core", 2, 1)(pair)
    encoder_grad, encoder_bias_grad = call(
        encoder_kernel,
        (sds((FEATS // 4, D), F32), sds((1, FEATS // 4), F32)),
        own, other, pair, near, positive,
        vmem=(0, 1, 2, 3, 4),
    )
    return encoder_grad.T, encoder_bias_grad[0], decoder_grad[None], bias_grad


def solution(mesh):
    split = Mesh(mesh.devices.reshape(4, 4, 4, 2, 2), FEAT + TGT)
    return jax.shard_map(
        body,
        mesh=split,
        in_specs=(
            P(FEAT, None),
            P(None, FEAT),
            P(FEAT),
            P(TGT, FEAT, None),
            P(TGT, None),
            P(TGT, FEAT, None),
        ),
        out_specs=(
            P(None, FEAT + TGT),
            P(FEAT + TGT),
            P(TGT, FEAT, None),
            P(TGT, None),
        ),
        check_vma=False,
    )
```

```python
import jax
import jax.numpy as jnp
import numpy as np
from jax import lax
from jax.experimental import pallas as pl
from jax.experimental.pallas import tpu as pltpu
from jax.sharding import Mesh, PartitionSpec as P

BF16 = jnp.bfloat16
F32 = jnp.float32
FEAT = ("zl", "y", "x")
TGT = ("zh", "core")
TN = (((0,), (0,)), ((), ()))
NT = (((1,), (1,)), ((), ()))
KEYS = (1, 2, 3)

J, ROWS, DEPTH, D, FEATS = 16, 3, 4, 4096, 256
COUNT = J * ROWS * DEPTH
WIDE, PIECE = D // 4, D // 16
HALF = D // 2


def call(kernel, outs, *args, vmem=(), **kwargs):
    args = [pltpu.with_memory_space_constraint(a, pltpu.VMEM) if i in vmem else a for i, a in enumerate(args)]
    return pl.pallas_call(
        kernel,
        out_shape=outs,
        compiler_params=pltpu.CompilerParams(vmem_limit_bytes=40 * 1024 * 1024),
        **kwargs,
    )(*args)


def coordinates():
    core, y, x = lax.axis_index("core"), lax.axis_index("y"), lax.axis_index("x")
    return jnp.where(core == 0, x, y), jnp.where(core == 0, y, x)


def columns(at, width):
    return pl.ds(pl.multiple_of(at * width, width), width)


def load_kernel(tokens_ref, enc_ref, tokens_out, enc_out, sems):
    copies = [
        pltpu.make_async_copy(tokens_ref, tokens_out, sems.at[0]),
        pltpu.make_async_copy(enc_ref, enc_out, sems.at[1]),
    ]
    for copy in copies:
        copy.start()
    for copy in copies:
        copy.wait()


def pack_kernel(own_ref, below_ref, above_ref, far_ref, out_ref):
    zl = lax.axis_index("zl")
    sub = lax.broadcasted_iota(jnp.int32, (8, WIDE), 0)
    sources = [(own_ref, 0), (below_ref, 3), (above_ref, 1), (far_ref, 2)]
    half = columns(lax.axis_index("core"), HALF)
    blocks = [(ref[:, half].astype(F32), (zl + step) % 4) for ref, step in sources]
    for i in range(ROWS):
        tile = jnp.zeros((8, WIDE), F32)
        for block, depth in blocks:
            for h in range(2):
                row = block[i : i + 1, h * WIDE : (h + 1) * WIDE]
                tile = jnp.where(sub == depth + 4 * h, row, tile)
        tile = tile.astype(BF16)
        for j in range(J):
            out_ref[j, 8 * i : 8 * i + 8, :] = tile


def forward_kernel(
    own_ref, other_ref, enc_ref, enc_bias_ref, dec_ref, target_ref,
    keep_ref, send1_ref, send2_ref, send3_ref, pos_ref, feats_ref, acc_ref,
):
    core, zl = lax.axis_index("core"), lax.axis_index("zl")
    member = lax.axis_index("y") * 4 + lax.axis_index("x")
    a, _ = coordinates()
    sums = []
    for h in range(2):
        sums.append(
            jnp.dot(own_ref[...], enc_ref[columns(2 * core + h, WIDE), :], preferred_element_type=F32)
            + jnp.dot(other_ref[...], enc_ref[columns(2 - 2 * core + h, WIDE), :], preferred_element_type=F32)
        )
    low, high = [s.reshape(COUNT // 8, 2, 8, FEATS) for s in sums]
    sub = lax.broadcasted_iota(jnp.int32, (COUNT // 8, 8, FEATS), 1)
    both = []
    for g in range(2):
        part = jnp.where(sub < 4, low[:, g], high[:, g])
        both.append(part + pltpu.roll(part, 4, 1))
    pre = jnp.where(sub < 4, both[0], both[1]).reshape(COUNT, FEATS) + enc_bias_ref[...]
    positive = jnp.maximum(pre, 0.0)
    pos_ref[...] = positive
    feats = (positive * positive).astype(BF16)
    feats_ref[...] = feats
    lane_sub = lax.broadcasted_iota(jnp.int32, (8, WIDE), 0)
    for key in (2, 1, 3, 0):
        out_ref = (keep_ref, send1_ref, send2_ref, send3_ref)[key]
        place = columns(a ^ key, WIDE)
        acc = keep_ref if key == 0 else acc_ref.at[key % 2]
        acc[...] = jnp.dot(feats, dec_ref[:, place], preferred_element_type=F32)
        values = target_ref[:, place].astype(F32)
        for i in range(ROWS):
            group = ROWS * member + i
            tile = pl.ds(pl.multiple_of(8 * (group // 2), 8), 8)
            row = 4 * (group % 2) + zl
            acc[tile, :] = acc[tile, :] - jnp.where(lane_sub == row, values[i : i + 1], 0.0)
        if key:
            out_ref[...] = acc[...].astype(BF16)


def middle_kernel(keep_ref, r1_ref, r2_ref, r3_ref, out_ref, send1_ref, send2_ref, send3_ref):
    _, b = coordinates()
    for key, ref in enumerate((out_ref, send1_ref, send2_ref, send3_ref)):
        place = columns(b ^ key, PIECE)
        total = (keep_ref[:, place] + r1_ref[:, place].astype(F32)) + (
            r2_ref[:, place].astype(F32) + r3_ref[:, place].astype(F32)
        )
        ref[...] = total.astype(ref.dtype)


def sum_kernel(keep_ref, r1_ref, r2_ref, r3_ref, out_ref):
    r1, r2, r3 = [ref[...].astype(F32) for ref in (r1_ref, r2_ref, r3_ref)]
    out_ref[...] = ((keep_ref[...] + r1) + (r2 + r3)).astype(BF16)


def error_kernel(own_ref, r1_ref, r2_ref, r3_ref, bias_ref, out_ref):
    a, b = coordinates()
    own, r1, r2, r3 = [ref[...].astype(F32) for ref in (own_ref, r1_ref, r2_ref, r3_ref)]
    bias = bias_ref[:, columns(4 * a + b, PIECE)]
    error = (((own + r1) + (r2 + r3)) + bias).astype(BF16)
    for j in range(J):
        out_ref[j] = error


def back_kernel(error_ref, dec_ref, keep_ref, send_ref):
    zh = lax.axis_index("zh")
    total = jnp.zeros((COUNT, FEATS), F32)
    for j in range(J):
        total = total + lax.dot_general(
            error_ref[j], dec_ref[:, j * PIECE : (j + 1) * PIECE], NT, preferred_element_type=F32
        )
    half = FEATS // 2
    keep_ref[...] = jnp.where(zh == 0, total[:, :half], total[:, half:])
    send_ref[...] = jnp.where(zh == 0, total[:, half:], total[:, :half]).astype(BF16)


def decoder_kernel(error_ref, feats_ref, grad_ref, bias_ref, done_ref, part_ref, sems):
    feats = feats_ref[...]
    copies = []
    for k in range(4):
        error = jnp.concatenate([error_ref[4 * k + j] for j in range(4)], axis=1)
        place = slice(k * WIDE, (k + 1) * WIDE)
        part_ref[k] = lax.dot_general(feats, error, TN, preferred_element_type=F32)
        copy = pltpu.make_async_copy(part_ref.at[k], grad_ref.at[:, place], sems.at[k])
        copy.start()
        copies.append(copy)
        bias_ref[:, place] = jnp.sum(error.astype(F32), axis=0, keepdims=True)
    done_ref[...] = jnp.zeros_like(done_ref)
    for copy in copies:
        copy.wait()


def pair_kernel(keep_ref, peer_ref, after_ref, out_ref):
    out_ref[...] = keep_ref[...] + peer_ref[...].astype(F32)


def encoder_kernel(own_ref, other_ref, pair_ref, near_ref, pos_ref, grad_ref, bias_ref):
    core, zh = lax.axis_index("core"), lax.axis_index("zh")
    quarter = FEATS // 4
    share = pair_ref[...] + near_ref[...]
    act = share * (2.0 * pos_ref[:, columns(zh, FEATS // 2)])
    act = jnp.where(core == 0, act[:, :quarter], act[:, quarter:])
    bias_ref[...] = jnp.sum(act, axis=0, keepdims=True)
    tiles = act.astype(BF16).astype(F32).reshape(COUNT // 8, 8, quarter)
    turned = pltpu.roll(tiles, 4, 1)
    sub = lax.broadcasted_iota(jnp.int32, tiles.shape, 1)
    zero = jnp.zeros_like(tiles)
    low = jnp.stack([jnp.where(sub < 4, tiles, zero), jnp.where(sub < 4, turned, zero)], axis=1)
    high = jnp.stack([jnp.where(sub < 4, zero, turned), jnp.where(sub < 4, zero, tiles)], axis=1)
    for h, side in enumerate((low, high)):
        side = side.reshape(2 * COUNT, quarter).astype(BF16)
        for ref, owner in ((own_ref, core), (other_ref, 1 - core)):
            grad_ref[:, columns(2 * owner + h, WIDE)] = lax.dot_general(
                side, ref[...], TN, preferred_element_type=F32
            )


def ring(step):
    index = lambda z: (z % 4) * 2 + z // 4
    return [(index(z), index((z + step) % 8)) for z in range(8)]


def mirror(x, axes, size, key):
    return lax.ppermute(x, axes, [(i, i ^ key) for i in range(size)])


def plane_swap(x, wide, key):
    pairs = []
    for i in range(32):
        y, x_at, core = i // 8, i // 2 % 4, i % 2
        along_x = wide == (core == 0)
        there = (y, x_at ^ key) if along_x else (y ^ key, x_at)
        pairs.append((i, 8 * there[0] + 2 * there[1] + core))
    return lax.ppermute(x, ("y", "x", "core"), pairs)


def plane_groups():
    ids = np.arange(256).reshape(4, 4, 4, 2, 2)
    return [
        [int(ids[(z, c % 4, c // 4) if core == 0 else (z, c // 4, c % 4)][zh, core]) for c in range(J)]
        for z, zh, core in np.ndindex(4, 2, 2)
    ]


def body(tokens, encoder_weight, encoder_bias, decoder_weight, decoder_bias, targets):
    sds, vmem = jax.ShapeDtypeStruct, pltpu.VMEM
    dec = decoder_weight[0]

    near_rows = [lax.ppermute(tokens, ("zl", "zh"), ring(step)) for step in (1, 7, 2)]
    tokens, encoder_weight = call(
        load_kernel,
        (vmem(tokens.shape, BF16), vmem(encoder_weight.shape, BF16)),
        tokens, encoder_weight,
        in_specs=[pl.BlockSpec(memory_space=pl.ANY)] * 2,
        scratch_shapes=[pltpu.SemaphoreType.DMA((2,))],
    )
    packed = call(pack_kernel, vmem((J, 8 * ROWS, WIDE), BF16), tokens, *near_rows, vmem=range(4))
    own = lax.all_to_all(packed, ("y", "x"), 0, 0, tiled=True)
    own = own.reshape(2 * COUNT, WIDE)
    other = mirror(own, "core", 2, 1)

    wide, piece = (COUNT, WIDE), (COUNT, PIECE)
    keep, *sends, positive, feats = call(
        forward_kernel,
        (vmem(wide, F32),) + (vmem(wide, BF16),) * 3 + (vmem((COUNT, FEATS), F32), vmem((COUNT, FEATS), BF16)),
        own, other, encoder_weight, encoder_bias[None], dec, targets[0],
        vmem=(0, 1, 2, 4),
        scratch_shapes=[vmem((2,) + wide, F32)],
    )
    moved = [plane_swap(sends[key - 1], True, key) for key in KEYS]
    keep, *sends = call(middle_kernel, (vmem(piece, F32),) + (vmem(piece, BF16),) * 3, keep, *moved, vmem=range(4))
    moved = [plane_swap(sends[key - 1], False, key) for key in KEYS]
    part = call(sum_kernel, vmem(piece, BF16), keep, *moved, vmem=range(4))
    moved = [mirror(part, "zl", DEPTH, key) for key in KEYS]
    copies = call(error_kernel, vmem((J,) + piece, BF16), part, *moved, decoder_bias, vmem=range(4))
    errors = lax.all_to_all(copies, FEAT + TGT, 0, 0, axis_index_groups=plane_groups(), tiled=True)

    half = (COUNT, FEATS // 2)
    keep, send = call(back_kernel, (vmem(half, F32), vmem(half, BF16)), errors, dec, vmem=range(2))
    peer = mirror(send, "zh", 2, 1)
    decoder_grad, bias_grad, done = call(
        decoder_kernel,
        (sds((FEATS, D), F32), sds((1, D), F32), vmem((8, 128), F32)),
        errors, feats,
        vmem=range(2),
        out_specs=(
            pl.BlockSpec(memory_space=pl.ANY),
            pl.BlockSpec(memory_space=pltpu.VMEM),
            pl.BlockSpec(memory_space=pltpu.VMEM),
        ),
        scratch_shapes=[vmem((4, FEATS, WIDE), F32), pltpu.SemaphoreType.DMA((4,))],
    )
    pair = call(pair_kernel, vmem(half, F32), keep, peer, done, vmem=range(3))
    near = mirror(pair, "core", 2, 1)
    encoder_grad, encoder_bias_grad = call(
        encoder_kernel,
        (sds((FEATS // 4, D), F32), sds((1, FEATS // 4), F32)),
        own, other, pair, near, positive,
        vmem=range(5),
    )
    return encoder_grad.T, encoder_bias_grad[0], decoder_grad[None], bias_grad


def solution(mesh):
    split = Mesh(mesh.devices.reshape(4, 4, 4, 2, 2), FEAT + TGT)
    return jax.shard_map(
        body,
        mesh=split,
        in_specs=(
            P(FEAT, None),
            P(None, FEAT),
            P(FEAT),
            P(TGT, FEAT, None),
            P(TGT, None),
            P(TGT, FEAT, None),
        ),
        out_specs=(
            P(None, FEAT + TGT),
            P(FEAT + TGT),
            P(TGT, FEAT, None),
            P(TGT, None),
        ),
        check_vma=False,
    )
```

```python
import jax
import jax.numpy as jnp
import numpy as np
from jax import lax
from jax.experimental import pallas as pl
from jax.experimental.pallas import tpu as pltpu
from jax.sharding import Mesh, PartitionSpec as P

BF16 = jnp.bfloat16
F32 = jnp.float32
FEAT = ("zl", "y", "x")
TGT = ("zh", "core")
TN = (((0,), (0,)), ((), ()))
NT = (((1,), (1,)), ((), ()))
KEYS = (1, 2, 3)

J, ROWS, DEPTH, D, FEATS = 16, 3, 4, 4096, 256
COUNT = J * ROWS * DEPTH
WIDE, PIECE = D // 4, D // 16
HALF = D // 2


def call(kernel, outs, *args, vmem=(), **kwargs):
    args = [pltpu.with_memory_space_constraint(a, pltpu.VMEM) if i in vmem else a for i, a in enumerate(args)]
    return pl.pallas_call(
        kernel,
        out_shape=outs,
        compiler_params=pltpu.CompilerParams(vmem_limit_bytes=40 * 1024 * 1024),
        **kwargs,
    )(*args)


def coordinates():
    core, y, x = lax.axis_index("core"), lax.axis_index("y"), lax.axis_index("x")
    return jnp.where(core == 0, x, y), jnp.where(core == 0, y, x)


def columns(at, width):
    return pl.ds(pl.multiple_of(at * width, width), width)


def load_kernel(tokens_ref, enc_ref, tokens_out, enc_out, sems):
    copies = [
        pltpu.make_async_copy(tokens_ref, tokens_out, sems.at[0]),
        pltpu.make_async_copy(enc_ref, enc_out, sems.at[1]),
    ]
    for copy in copies:
        copy.start()
    for copy in copies:
        copy.wait()


def pack_kernel(own_ref, below_ref, above_ref, far_ref, out_ref):
    zl = lax.axis_index("zl")
    sub = lax.broadcasted_iota(jnp.int32, (8, WIDE), 0)
    sources = [(own_ref, 0), (below_ref, 3), (above_ref, 1), (far_ref, 2)]
    half = columns(lax.axis_index("core"), HALF)
    blocks = [(ref[:, half].astype(F32), (zl + step) % 4) for ref, step in sources]
    for i in range(ROWS):
        tile = jnp.zeros((8, WIDE), F32)
        for block, depth in blocks:
            for h in range(2):
                row = block[i : i + 1, h * WIDE : (h + 1) * WIDE]
                tile = jnp.where(sub == depth + 4 * h, row, tile)
        tile = tile.astype(BF16)
        for j in range(J):
            out_ref[j, 8 * i : 8 * i + 8, :] = tile


def forward_kernel(
    own_ref, other_ref, enc_ref, enc_bias_ref, dec_ref, target_ref,
    send2_ref, pos_ref, feats_ref, acc_ref,
):
    core = lax.axis_index("core")
    a, _ = coordinates()
    sums = []
    for h in range(2):
        sums.append(
            jnp.dot(own_ref[...], enc_ref[columns(2 * core + h, WIDE), :], preferred_element_type=F32)
            + jnp.dot(other_ref[...], enc_ref[columns(2 - 2 * core + h, WIDE), :], preferred_element_type=F32)
        )
    low, high = [s.reshape(COUNT // 8, 2, 8, FEATS) for s in sums]
    sub = lax.broadcasted_iota(jnp.int32, (COUNT // 8, 8, FEATS), 1)
    both = []
    for g in range(2):
        part = jnp.where(sub < 4, low[:, g], high[:, g])
        both.append(part + pltpu.roll(part, 4, 1))
    pre = jnp.where(sub < 4, both[0], both[1]).reshape(COUNT, FEATS) + enc_bias_ref[...]
    positive = jnp.maximum(pre, 0.0)
    pos_ref[...] = positive
    feats = (positive * positive).astype(BF16)
    feats_ref[...] = feats
    product(feats, dec_ref, target_ref, a ^ 2, acc_ref)
    send2_ref[...] = acc_ref[...].astype(BF16)


def product(feats, dec_ref, target_ref, at, acc_ref):
    zl, member = lax.axis_index("zl"), lax.axis_index("y") * 4 + lax.axis_index("x")
    lane_sub = lax.broadcasted_iota(jnp.int32, (8, WIDE), 0)
    place = columns(at, WIDE)
    acc_ref[...] = jnp.dot(feats, dec_ref[:, place], preferred_element_type=F32)
    values = target_ref[:, place].astype(F32)
    for i in range(ROWS):
        group = ROWS * member + i
        tile = pl.ds(pl.multiple_of(8 * (group // 2), 8), 8)
        row = 4 * (group % 2) + zl
        acc_ref[tile, :] = acc_ref[tile, :] - jnp.where(lane_sub == row, values[i : i + 1], 0.0)


def rest_kernel(feats_ref, dec_ref, target_ref, keep_ref, send1_ref, send3_ref, acc_ref):
    a, _ = coordinates()
    for key, out_ref in ((1, send1_ref), (3, send3_ref)):
        product(feats_ref[...], dec_ref, target_ref, a ^ key, acc_ref.at[key // 2])
        out_ref[...] = acc_ref[key // 2].astype(BF16)
    product(feats_ref[...], dec_ref, target_ref, a, keep_ref)


def middle_kernel(keep_ref, r1_ref, r2_ref, r3_ref, out_ref, send1_ref, send2_ref, send3_ref):
    _, b = coordinates()
    for key, ref in enumerate((out_ref, send1_ref, send2_ref, send3_ref)):
        place = columns(b ^ key, PIECE)
        total = (keep_ref[:, place] + r1_ref[:, place].astype(F32)) + (
            r2_ref[:, place].astype(F32) + r3_ref[:, place].astype(F32)
        )
        ref[...] = total.astype(ref.dtype)


def sum_kernel(keep_ref, r2_ref, r1_ref, r3_ref, out_ref):
    r1, r2, r3 = [ref[...].astype(F32) for ref in (r1_ref, r2_ref, r3_ref)]
    out_ref[...] = ((keep_ref[...] + r1) + (r2 + r3)).astype(BF16)


def error_kernel(own_ref, r2_ref, r3_ref, r1_ref, bias_ref, out_ref):
    a, b = coordinates()
    own, r1, r2, r3 = [ref[...].astype(F32) for ref in (own_ref, r1_ref, r2_ref, r3_ref)]
    bias = bias_ref[:, columns(4 * a + b, PIECE)]
    error = (((own + r1) + (r2 + r3)) + bias).astype(BF16)
    for j in range(J):
        out_ref[j] = error


def back_half(error_ref, dec_ref, side):
    rows = columns(side, FEATS // 2)
    total = jnp.zeros((COUNT, FEATS // 2), F32)
    for j in range(J):
        total = total + lax.dot_general(
            error_ref[j], dec_ref[rows, j * PIECE : (j + 1) * PIECE], NT, preferred_element_type=F32
        )
    return total


def send_kernel(error_ref, dec_ref, out_ref):
    out_ref[...] = back_half(error_ref, dec_ref, 1 - lax.axis_index("zh")).astype(BF16)


def keep_kernel(error_ref, dec_ref, out_ref):
    out_ref[...] = back_half(error_ref, dec_ref, lax.axis_index("zh"))


def decoder_kernel(error_ref, feats_ref, grad_ref, bias_ref, done_ref, part_ref, sems):
    feats = feats_ref[...]
    copies = []
    for k in range(4):
        error = jnp.concatenate([error_ref[4 * k + j] for j in range(4)], axis=1)
        place = slice(k * WIDE, (k + 1) * WIDE)
        part_ref[k] = lax.dot_general(feats, error, TN, preferred_element_type=F32)
        copy = pltpu.make_async_copy(part_ref.at[k], grad_ref.at[:, place], sems.at[k])
        copy.start()
        copies.append(copy)
        bias_ref[:, place] = jnp.sum(error.astype(F32), axis=0, keepdims=True)
    done_ref[...] = jnp.zeros_like(done_ref)
    for copy in copies:
        copy.wait()


def pair_kernel(keep_ref, peer_ref, after_ref, out_ref):
    out_ref[...] = keep_ref[...] + peer_ref[...].astype(F32)


def encoder_kernel(own_ref, other_ref, pair_ref, near_ref, pos_ref, grad_ref, bias_ref):
    core, zh = lax.axis_index("core"), lax.axis_index("zh")
    quarter = FEATS // 4
    share = pair_ref[...] + near_ref[...]
    act = share * (2.0 * pos_ref[:, columns(zh, FEATS // 2)])
    act = jnp.where(core == 0, act[:, :quarter], act[:, quarter:])
    bias_ref[...] = jnp.sum(act, axis=0, keepdims=True)
    tiles = act.astype(BF16).astype(F32).reshape(COUNT // 8, 8, quarter)
    turned = pltpu.roll(tiles, 4, 1)
    sub = lax.broadcasted_iota(jnp.int32, tiles.shape, 1)
    zero = jnp.zeros_like(tiles)
    low = jnp.stack([jnp.where(sub < 4, tiles, zero), jnp.where(sub < 4, turned, zero)], axis=1)
    high = jnp.stack([jnp.where(sub < 4, zero, turned), jnp.where(sub < 4, zero, tiles)], axis=1)
    for h, side in enumerate((low, high)):
        side = side.reshape(2 * COUNT, quarter).astype(BF16)
        for ref, owner in ((own_ref, core), (other_ref, 1 - core)):
            grad_ref[:, columns(2 * owner + h, WIDE)] = lax.dot_general(
                side, ref[...], TN, preferred_element_type=F32
            )


def ring(step):
    index = lambda z: (z % 4) * 2 + z // 4
    return [(index(z), index((z + step) % 8)) for z in range(8)]


def mirror(x, axes, size, key):
    return lax.ppermute(x, axes, [(i, i ^ key) for i in range(size)])


def plane_swap(x, wide, key):
    pairs = []
    for i in range(32):
        y, x_at, core = i // 8, i // 2 % 4, i % 2
        along_x = wide == (core == 0)
        there = (y, x_at ^ key) if along_x else (y ^ key, x_at)
        pairs.append((i, 8 * there[0] + 2 * there[1] + core))
    return lax.ppermute(x, ("y", "x", "core"), pairs)


def plane_groups():
    ids = np.arange(256).reshape(4, 4, 4, 2, 2)
    return [
        [int(ids[(z, c % 4, c // 4) if core == 0 else (z, c // 4, c % 4)][zh, core]) for c in range(J)]
        for z, zh, core in np.ndindex(4, 2, 2)
    ]


def body(tokens, encoder_weight, encoder_bias, decoder_weight, decoder_bias, targets):
    sds, vmem = jax.ShapeDtypeStruct, pltpu.VMEM
    dec = decoder_weight[0]

    far_rows, *near_rows = [lax.ppermute(tokens, ("zl", "zh"), ring(step)) for step in (2, 1, 7)]
    tokens, encoder_weight = call(
        load_kernel,
        (vmem(tokens.shape, BF16), vmem(encoder_weight.shape, BF16)),
        tokens, encoder_weight,
        in_specs=[pl.BlockSpec(memory_space=pl.ANY)] * 2,
        scratch_shapes=[pltpu.SemaphoreType.DMA((2,))],
    )
    packed = call(pack_kernel, vmem((J, 8 * ROWS, WIDE), BF16), tokens, *near_rows, far_rows, vmem=range(4))
    own = lax.all_to_all(packed, ("y", "x"), 0, 0, tiled=True)
    own = own.reshape(2 * COUNT, WIDE)
    other = mirror(own, "core", 2, 1)

    wide, piece = (COUNT, WIDE), (COUNT, PIECE)
    send2, positive, feats = call(
        forward_kernel,
        (vmem(wide, BF16), vmem((COUNT, FEATS), F32), vmem((COUNT, FEATS), BF16)),
        own, other, encoder_weight, encoder_bias[None], dec, targets[0],
        vmem=(0, 1, 2, 4, 5),
        scratch_shapes=[vmem(wide, F32)],
    )
    moved2 = plane_swap(send2, True, 2)
    keep, send1, send3 = call(
        rest_kernel,
        (vmem(wide, F32), vmem(wide, BF16), vmem(wide, BF16)),
        feats, dec, targets[0],
        vmem=range(3),
        scratch_shapes=[vmem((2,) + wide, F32)],
    )
    moved = [plane_swap(send1, True, 1), moved2, plane_swap(send3, True, 3)]
    keep, *sends = call(middle_kernel, (vmem(piece, F32),) + (vmem(piece, BF16),) * 3, keep, *moved, vmem=range(4))
    moved = [plane_swap(sends[key - 1], False, key) for key in (2, 1, 3)]
    part = call(sum_kernel, vmem(piece, BF16), keep, *moved, vmem=range(4))
    moved = [mirror(part, "zl", DEPTH, key) for key in (2, 3, 1)]
    copies = call(error_kernel, vmem((J,) + piece, BF16), part, *moved, decoder_bias, vmem=range(4))
    errors = lax.all_to_all(copies, FEAT + TGT, 0, 0, axis_index_groups=plane_groups(), tiled=True)

    half = (COUNT, FEATS // 2)
    send = call(send_kernel, vmem(half, BF16), errors, dec, vmem=range(2))
    peer = mirror(send, "zh", 2, 1)
    keep = call(keep_kernel, vmem(half, F32), errors, dec, vmem=range(2))
    decoder_grad, bias_grad, done = call(
        decoder_kernel,
        (sds((FEATS, D), F32), sds((1, D), F32), vmem((8, 128), F32)),
        errors, feats,
        vmem=range(2),
        out_specs=(
            pl.BlockSpec(memory_space=pl.ANY),
            pl.BlockSpec(memory_space=pltpu.VMEM),
            pl.BlockSpec(memory_space=pltpu.VMEM),
        ),
        scratch_shapes=[vmem((4, FEATS, WIDE), F32), pltpu.SemaphoreType.DMA((4,))],
    )
    pair = call(pair_kernel, vmem(half, F32), keep, peer, done, vmem=range(3))
    near = mirror(pair, "core", 2, 1)
    encoder_grad, encoder_bias_grad = call(
        encoder_kernel,
        (sds((FEATS // 4, D), F32), sds((1, FEATS // 4), F32)),
        own, other, pair, near, positive,
        vmem=range(5),
    )
    return encoder_grad.T, encoder_bias_grad[0], decoder_grad[None], bias_grad


def solution(mesh):
    split = Mesh(mesh.devices.reshape(4, 4, 4, 2, 2), FEAT + TGT)
    return jax.shard_map(
        body,
        mesh=split,
        in_specs=(
            P(FEAT, None),
            P(None, FEAT),
            P(FEAT),
            P(TGT, FEAT, None),
            P(TGT, None),
            P(TGT, FEAT, None),
        ),
        out_specs=(
            P(None, FEAT + TGT),
            P(FEAT + TGT),
            P(TGT, FEAT, None),
            P(TGT, None),
        ),
        check_vma=False,
    )
```

```python
import jax
import jax.numpy as jnp
from jax import lax
from jax.experimental import pallas as pl
from jax.experimental.pallas import tpu as pltpu
from jax.sharding import Mesh, PartitionSpec as P

BF16 = jnp.bfloat16
F32 = jnp.float32
FEAT = ("zl", "y", "x")
TGT = ("zh", "core")
TN = (((0,), (0,)), ((), ()))
NT = (((1,), (1,)), ((), ()))
KEYS = (1, 2, 3)

J, ROWS, DEPTH, D, FEATS = 16, 3, 4, 4096, 256
COUNT = J * ROWS * DEPTH
WIDE, PIECE = D // 4, D // 16
HALF = D // 2


def call(kernel, outs, *args, vmem=(), **kwargs):
    args = [pltpu.with_memory_space_constraint(a, pltpu.VMEM) if i in vmem else a for i, a in enumerate(args)]
    return pl.pallas_call(
        kernel,
        out_shape=outs,
        compiler_params=pltpu.CompilerParams(vmem_limit_bytes=40 * 1024 * 1024),
        **kwargs,
    )(*args)


def coordinates():
    core, y, x = lax.axis_index("core"), lax.axis_index("y"), lax.axis_index("x")
    return jnp.where(core == 0, x, y), jnp.where(core == 0, y, x)


def columns(at, width):
    return pl.ds(pl.multiple_of(at * width, width), width)


def load_kernel(tokens_ref, enc_ref, tokens_out, enc_out, sems):
    copies = [
        pltpu.make_async_copy(tokens_ref, tokens_out, sems.at[0]),
        pltpu.make_async_copy(enc_ref, enc_out, sems.at[1]),
    ]
    for copy in copies:
        copy.start()
    for copy in copies:
        copy.wait()


def pack_kernel(own_ref, far_ref, below_ref, above_ref, out_ref):
    zl = lax.axis_index("zl")
    sub = lax.broadcasted_iota(jnp.int32, (8, WIDE), 0)
    sources = [(own_ref, 0), (below_ref, 3), (above_ref, 1), (far_ref, 2)]
    half = columns(lax.axis_index("core"), HALF)
    blocks = [(ref[:, half].astype(F32), (zl + step) % 4) for ref, step in sources]
    for i in range(ROWS):
        tile = jnp.zeros((8, WIDE), F32)
        for block, depth in blocks:
            for h in range(2):
                row = block[i : i + 1, h * WIDE : (h + 1) * WIDE]
                tile = jnp.where(sub == depth + 4 * h, row, tile)
        tile = tile.astype(BF16)
        for j in range(J):
            out_ref[j, 8 * i : 8 * i + 8, :] = tile


def forward_kernel(
    own_ref, other_ref, enc_ref, enc_bias_ref, dec_ref, target_ref,
    send2_ref, pos_ref, feats_ref, acc_ref,
):
    core = lax.axis_index("core")
    a, _ = coordinates()
    sums = []
    for h in range(2):
        sums.append(
            jnp.dot(own_ref[...], enc_ref[columns(2 * core + h, WIDE), :], preferred_element_type=F32)
            + jnp.dot(other_ref[...], enc_ref[columns(2 - 2 * core + h, WIDE), :], preferred_element_type=F32)
        )
    low, high = [s.reshape(COUNT // 8, 2, 8, FEATS) for s in sums]
    sub = lax.broadcasted_iota(jnp.int32, (COUNT // 8, 8, FEATS), 1)
    both = []
    for g in range(2):
        part = jnp.where(sub < 4, low[:, g], high[:, g])
        both.append(part + pltpu.roll(part, 4, 1))
    pre = jnp.where(sub < 4, both[0], both[1]).reshape(COUNT, FEATS) + enc_bias_ref[...]
    positive = jnp.maximum(pre, 0.0)
    pos_ref[...] = positive
    feats = (positive * positive).astype(BF16)
    feats_ref[...] = feats
    product(feats, dec_ref, target_ref, a ^ 2, acc_ref)
    send2_ref[...] = acc_ref[...].astype(BF16)


def product(feats, dec_ref, target_ref, at, acc_ref):
    zl, member = lax.axis_index("zl"), lax.axis_index("y") * 4 + lax.axis_index("x")
    lane_sub = lax.broadcasted_iota(jnp.int32, (8, WIDE), 0)
    place = columns(at, WIDE)
    acc_ref[...] = jnp.dot(feats, dec_ref[:, place], preferred_element_type=F32)
    values = target_ref[:, place].astype(F32)
    for i in range(ROWS):
        group = ROWS * member + i
        tile = pl.ds(pl.multiple_of(8 * (group // 2), 8), 8)
        row = 4 * (group % 2) + zl
        acc_ref[tile, :] = acc_ref[tile, :] - jnp.where(lane_sub == row, values[i : i + 1], 0.0)


def rest_kernel(feats_ref, dec_ref, target_ref, keep_ref, send1_ref, send3_ref, acc_ref):
    a, _ = coordinates()
    for key, out_ref in ((1, send1_ref), (3, send3_ref)):
        product(feats_ref[...], dec_ref, target_ref, a ^ key, acc_ref.at[key // 2])
        out_ref[...] = acc_ref[key // 2].astype(BF16)
    product(feats_ref[...], dec_ref, target_ref, a, keep_ref)


def middle_kernel(keep_ref, r1_ref, r2_ref, r3_ref, out_ref, send1_ref, send2_ref, send3_ref):
    _, b = coordinates()
    for key, ref in enumerate((out_ref, send1_ref, send2_ref, send3_ref)):
        place = columns(b ^ key, PIECE)
        total = (keep_ref[:, place] + r1_ref[:, place].astype(F32)) + (
            r2_ref[:, place].astype(F32) + r3_ref[:, place].astype(F32)
        )
        ref[...] = total.astype(ref.dtype)


def sum_kernel(keep_ref, r2_ref, r1_ref, r3_ref, out_ref):
    r1, r2, r3 = [ref[...].astype(F32) for ref in (r1_ref, r2_ref, r3_ref)]
    out_ref[...] = ((keep_ref[...] + r1) + (r2 + r3)).astype(BF16)


def error_kernel(own_ref, r2_ref, r3_ref, r1_ref, bias_ref, out_ref):
    a, b = coordinates()
    own, r1, r2, r3 = [ref[...].astype(F32) for ref in (own_ref, r1_ref, r2_ref, r3_ref)]
    bias = bias_ref[:, columns(4 * a + b, PIECE)]
    out_ref[...] = (((own + r1) + (r2 + r3)) + bias).astype(BF16)


def widen_kernel(own_ref, r2_ref, r1_ref, r3_ref, out_ref):
    _, b = coordinates()
    for key, ref in ((0, own_ref), (1, r1_ref), (2, r2_ref), (3, r3_ref)):
        out_ref[:, columns(b ^ key, PIECE)] = ref[...]


def back_half(blocks, dec_ref, side):
    a, _ = coordinates()
    rows = columns(side, FEATS // 2)
    total = jnp.zeros((COUNT, FEATS // 2), F32)
    for key, ref in zip((0, 1, 3, 2), blocks):
        total = total + lax.dot_general(
            ref[...], dec_ref[rows, columns(a ^ key, WIDE)], NT, preferred_element_type=F32
        )
    return total


def send_kernel(own_ref, r1_ref, r3_ref, r2_ref, dec_ref, out_ref):
    blocks = (own_ref, r1_ref, r3_ref, r2_ref)
    out_ref[...] = back_half(blocks, dec_ref, 1 - lax.axis_index("zh")).astype(BF16)


def keep_kernel(own_ref, r1_ref, r3_ref, r2_ref, dec_ref, out_ref):
    out_ref[...] = back_half((own_ref, r1_ref, r3_ref, r2_ref), dec_ref, lax.axis_index("zh"))


def decoder_kernel(own_ref, r1_ref, r3_ref, r2_ref, feats_ref, grad_ref, bias_ref, done_ref, part_ref, row_ref, sems):
    a, _ = coordinates()
    feats = feats_ref[...]
    copies = []
    for key, ref in ((0, own_ref), (1, r1_ref), (3, r3_ref), (2, r2_ref)):
        place = columns(a ^ key, WIDE)
        part_ref[key] = lax.dot_general(feats, ref[...], TN, preferred_element_type=F32)
        copy = pltpu.make_async_copy(part_ref.at[key], grad_ref.at[:, place], sems.at[key])
        copy.start()
        copies.append(copy)
        row_ref[:, place] = jnp.sum(ref[...].astype(F32), axis=0, keepdims=True)
    copy = pltpu.make_async_copy(row_ref, bias_ref, sems.at[4])
    copy.start()
    copies.append(copy)
    done_ref[...] = jnp.zeros_like(done_ref)
    for copy in copies:
        copy.wait()


def pair_kernel(keep_ref, peer_ref, after_ref, out_ref):
    out_ref[...] = keep_ref[...] + peer_ref[...].astype(F32)


def encoder_kernel(own_ref, other_ref, pair_ref, near_ref, pos_ref, grad_ref, bias_ref):
    core, zh = lax.axis_index("core"), lax.axis_index("zh")
    quarter = FEATS // 4
    share = pair_ref[...] + near_ref[...]
    act = share * (2.0 * pos_ref[:, columns(zh, FEATS // 2)])
    act = jnp.where(core == 0, act[:, :quarter], act[:, quarter:])
    bias_ref[...] = jnp.sum(act, axis=0, keepdims=True)
    tiles = act.astype(BF16).astype(F32).reshape(COUNT // 8, 8, quarter)
    turned = pltpu.roll(tiles, 4, 1)
    sub = lax.broadcasted_iota(jnp.int32, tiles.shape, 1)
    zero = jnp.zeros_like(tiles)
    low = jnp.stack([jnp.where(sub < 4, tiles, zero), jnp.where(sub < 4, turned, zero)], axis=1)
    high = jnp.stack([jnp.where(sub < 4, zero, turned), jnp.where(sub < 4, zero, tiles)], axis=1)
    for h, side in enumerate((low, high)):
        side = side.reshape(2 * COUNT, quarter).astype(BF16)
        for ref, owner in ((own_ref, core), (other_ref, 1 - core)):
            grad_ref[:, columns(2 * owner + h, WIDE)] = lax.dot_general(
                side, ref[...], TN, preferred_element_type=F32
            )


def ring(step):
    index = lambda z: (z % 4) * 2 + z // 4
    return [(index(z), index((z + step) % 8)) for z in range(8)]


def mirror(x, axes, size, key):
    return lax.ppermute(x, axes, [(i, i ^ key) for i in range(size)])


def plane_swap(x, wide, key):
    pairs = []
    for i in range(32):
        y, x_at, core = i // 8, i // 2 % 4, i % 2
        along_x = wide == (core == 0)
        there = (y, x_at ^ key) if along_x else (y ^ key, x_at)
        pairs.append((i, 8 * there[0] + 2 * there[1] + core))
    return lax.ppermute(x, ("y", "x", "core"), pairs)


def body(tokens, encoder_weight, encoder_bias, decoder_weight, decoder_bias, targets):
    sds, vmem = jax.ShapeDtypeStruct, pltpu.VMEM
    dec = decoder_weight[0]

    far_rows, *near_rows = [lax.ppermute(tokens, ("zl", "zh"), ring(step)) for step in (2, 1, 7)]
    tokens, encoder_weight = call(
        load_kernel,
        (vmem(tokens.shape, BF16), vmem(encoder_weight.shape, BF16)),
        tokens, encoder_weight,
        in_specs=[pl.BlockSpec(memory_space=pl.ANY)] * 2,
        scratch_shapes=[pltpu.SemaphoreType.DMA((2,))],
    )
    packed = call(pack_kernel, vmem((J, 8 * ROWS, WIDE), BF16), tokens, far_rows, *near_rows, vmem=range(4))
    own = lax.all_to_all(packed, ("y", "x"), 0, 0, tiled=True)
    own = own.reshape(2 * COUNT, WIDE)
    other = mirror(own, "core", 2, 1)

    wide, piece = (COUNT, WIDE), (COUNT, PIECE)
    send2, positive, feats = call(
        forward_kernel,
        (vmem(wide, BF16), vmem((COUNT, FEATS), F32), vmem((COUNT, FEATS), BF16)),
        own, other, encoder_weight, encoder_bias[None], dec, targets[0],
        vmem=(0, 1, 2, 4, 5),
        scratch_shapes=[vmem(wide, F32)],
    )
    moved2 = plane_swap(send2, True, 2)
    keep, send1, send3 = call(
        rest_kernel,
        (vmem(wide, F32), vmem(wide, BF16), vmem(wide, BF16)),
        feats, dec, targets[0],
        vmem=range(3),
        scratch_shapes=[vmem((2,) + wide, F32)],
    )
    moved = [plane_swap(send1, True, 1), moved2, plane_swap(send3, True, 3)]
    keep, *sends = call(middle_kernel, (vmem(piece, F32),) + (vmem(piece, BF16),) * 3, keep, *moved, vmem=range(4))
    moved = [plane_swap(sends[key - 1], False, key) for key in (2, 1, 3)]
    part = call(sum_kernel, vmem(piece, BF16), keep, *moved, vmem=range(4))
    moved = [mirror(part, "zl", DEPTH, key) for key in (2, 3, 1)]
    error = call(error_kernel, vmem(piece, BF16), part, *moved, decoder_bias, vmem=range(4))
    moved = [plane_swap(error, False, key) for key in (2, 1, 3)]
    block = call(widen_kernel, vmem(wide, BF16), error, *moved, vmem=range(4))
    errors = [block] + [plane_swap(block, True, key) for key in (1, 3, 2)]

    half = (COUNT, FEATS // 2)
    send = call(send_kernel, vmem(half, BF16), *errors, dec, vmem=range(5))
    peer = mirror(send, "zh", 2, 1)
    keep = call(keep_kernel, vmem(half, F32), *errors, dec, vmem=range(5))
    decoder_grad, bias_grad, done = call(
        decoder_kernel,
        (sds((FEATS, D), F32), sds((1, D), F32), vmem((8, 128), F32)),
        *errors, feats,
        vmem=range(5),
        out_specs=(
            pl.BlockSpec(memory_space=pl.ANY),
            pl.BlockSpec(memory_space=pl.ANY),
            pl.BlockSpec(memory_space=pltpu.VMEM),
        ),
        scratch_shapes=[vmem((4, FEATS, WIDE), F32), vmem((1, D), F32), pltpu.SemaphoreType.DMA((5,))],
    )
    pair = call(pair_kernel, vmem(half, F32), keep, peer, done, vmem=range(3))
    near = mirror(pair, "core", 2, 1)
    encoder_grad, encoder_bias_grad = call(
        encoder_kernel,
        (sds((FEATS // 4, D), F32), sds((1, FEATS // 4), F32)),
        own, other, pair, near, positive,
        vmem=range(5),
    )
    return encoder_grad.T, encoder_bias_grad[0], decoder_grad[None], bias_grad


def solution(mesh):
    split = Mesh(mesh.devices.reshape(4, 4, 4, 2, 2), FEAT + TGT)
    return jax.shard_map(
        body,
        mesh=split,
        in_specs=(
            P(FEAT, None),
            P(None, FEAT),
            P(FEAT),
            P(TGT, FEAT, None),
            P(TGT, None),
            P(TGT, FEAT, None),
        ),
        out_specs=(
            P(None, FEAT + TGT),
            P(FEAT + TGT),
            P(TGT, FEAT, None),
            P(TGT, None),
        ),
        check_vma=False,
    )
```

```python
import jax
import jax.numpy as jnp
import numpy as np
from jax import lax
from jax.experimental import pallas as pl
from jax.experimental.pallas import tpu as pltpu
from jax.sharding import Mesh, PartitionSpec as P

BF16 = jnp.bfloat16
F32 = jnp.float32
FEAT = ("zl", "y", "x")
TGT = ("zh", "core")
TN = (((0,), (0,)), ((), ()))
NT = (((1,), (1,)), ((), ()))
KEYS = (1, 2, 3)

J, ROWS, DEPTH, D, FEATS = 16, 3, 4, 4096, 256
COUNT = J * ROWS * DEPTH
WIDE, PIECE = D // 4, D // 16
HALF = D // 2


def call(kernel, outs, *args, vmem=(), **kwargs):
    args = [pltpu.with_memory_space_constraint(a, pltpu.VMEM) if i in vmem else a for i, a in enumerate(args)]
    return pl.pallas_call(
        kernel,
        out_shape=outs,
        compiler_params=pltpu.CompilerParams(vmem_limit_bytes=40 * 1024 * 1024),
        **kwargs,
    )(*args)


def coordinates():
    core, y, x = lax.axis_index("core"), lax.axis_index("y"), lax.axis_index("x")
    return jnp.where(core == 0, x, y), jnp.where(core == 0, y, x)


def columns(at, width):
    return pl.ds(pl.multiple_of(at * width, width), width)


def load_kernel(tokens_ref, enc_ref, tokens_out, enc_out, sems):
    copies = [
        pltpu.make_async_copy(tokens_ref, tokens_out, sems.at[0]),
        pltpu.make_async_copy(enc_ref, enc_out, sems.at[1]),
    ]
    for copy in copies:
        copy.start()
    for copy in copies:
        copy.wait()


def pack_kernel(own_ref, far_ref, below_ref, above_ref, out_ref):
    zl = lax.axis_index("zl")
    sub = lax.broadcasted_iota(jnp.int32, (8, WIDE), 0)
    sources = [(own_ref, 0), (below_ref, 3), (above_ref, 1), (far_ref, 2)]
    half = columns(lax.axis_index("core"), HALF)
    blocks = [(ref[:, half].astype(F32), (zl + step) % 4) for ref, step in sources]
    for i in range(ROWS):
        tile = jnp.zeros((8, WIDE), F32)
        for block, depth in blocks:
            for h in range(2):
                row = block[i : i + 1, h * WIDE : (h + 1) * WIDE]
                tile = jnp.where(sub == depth + 4 * h, row, tile)
        tile = tile.astype(BF16)
        for j in range(J):
            out_ref[j, 8 * i : 8 * i + 8, :] = tile


def forward_kernel(
    own_ref, other_ref, enc_ref, enc_bias_ref, dec_ref, target_ref,
    send2_ref, pos_ref, feats_ref, acc_ref,
):
    core = lax.axis_index("core")
    a, _ = coordinates()
    sums = []
    for h in range(2):
        sums.append(
            jnp.dot(own_ref[...], enc_ref[columns(2 * core + h, WIDE), :], preferred_element_type=F32)
            + jnp.dot(other_ref[...], enc_ref[columns(2 - 2 * core + h, WIDE), :], preferred_element_type=F32)
        )
    low, high = [s.reshape(COUNT // 8, 2, 8, FEATS) for s in sums]
    sub = lax.broadcasted_iota(jnp.int32, (COUNT // 8, 8, FEATS), 1)
    both = []
    for g in range(2):
        part = jnp.where(sub < 4, low[:, g], high[:, g])
        both.append(part + pltpu.roll(part, 4, 1))
    pre = jnp.where(sub < 4, both[0], both[1]).reshape(COUNT, FEATS) + enc_bias_ref[...]
    positive = jnp.maximum(pre, 0.0)
    pos_ref[...] = positive
    feats = (positive * positive).astype(BF16)
    feats_ref[...] = feats
    product(feats, dec_ref, target_ref, a ^ 2, acc_ref)
    send2_ref[...] = acc_ref[...].astype(BF16)


def product(feats, dec_ref, target_ref, at, acc_ref):
    zl, member = lax.axis_index("zl"), lax.axis_index("y") * 4 + lax.axis_index("x")
    lane_sub = lax.broadcasted_iota(jnp.int32, (8, WIDE), 0)
    place = columns(at, WIDE)
    acc_ref[...] = jnp.dot(feats, dec_ref[:, place], preferred_element_type=F32)
    values = target_ref[:, place].astype(F32)
    for i in range(ROWS):
        group = ROWS * member + i
        tile = pl.ds(pl.multiple_of(8 * (group // 2), 8), 8)
        row = 4 * (group % 2) + zl
        acc_ref[tile, :] = acc_ref[tile, :] - jnp.where(lane_sub == row, values[i : i + 1], 0.0)


def rest_kernel(feats_ref, dec_ref, target_ref, keep_ref, send1_ref, send3_ref, acc_ref):
    a, _ = coordinates()
    for key, out_ref in ((1, send1_ref), (3, send3_ref)):
        product(feats_ref[...], dec_ref, target_ref, a ^ key, acc_ref.at[key // 2])
        out_ref[...] = acc_ref[key // 2].astype(BF16)
    product(feats_ref[...], dec_ref, target_ref, a, keep_ref)


def middle_kernel(keep_ref, r1_ref, r2_ref, r3_ref, out_ref, send1_ref, send2_ref, send3_ref):
    _, b = coordinates()
    for key, ref in enumerate((out_ref, send1_ref, send2_ref, send3_ref)):
        place = columns(b ^ key, PIECE)
        total = (keep_ref[:, place] + r1_ref[:, place].astype(F32)) + (
            r2_ref[:, place].astype(F32) + r3_ref[:, place].astype(F32)
        )
        ref[...] = total.astype(ref.dtype)


def sum_kernel(keep_ref, r2_ref, r1_ref, r3_ref, out_ref):
    r1, r2, r3 = [ref[...].astype(F32) for ref in (r1_ref, r2_ref, r3_ref)]
    out_ref[...] = ((keep_ref[...] + r1) + (r2 + r3)).astype(BF16)


def error_kernel(own_ref, r2_ref, r3_ref, r1_ref, bias_ref, out_ref):
    a, b = coordinates()
    own, r1, r2, r3 = [ref[...].astype(F32) for ref in (own_ref, r1_ref, r2_ref, r3_ref)]
    bias = bias_ref[:, columns(4 * a + b, PIECE)]
    error = (((own + r1) + (r2 + r3)) + bias).astype(BF16)
    for j in range(J):
        out_ref[j] = error


def back_half(error_ref, dec_ref, side):
    rows = columns(side, FEATS // 2)
    total = jnp.zeros((COUNT, FEATS // 2), F32)
    for j in range(J):
        total = total + lax.dot_general(
            error_ref[j], dec_ref[rows, j * PIECE : (j + 1) * PIECE], NT, preferred_element_type=F32
        )
    return total


def send_kernel(error_ref, dec_ref, out_ref):
    out_ref[...] = back_half(error_ref, dec_ref, 1 - lax.axis_index("zh")).astype(BF16)


def keep_kernel(error_ref, dec_ref, out_ref):
    out_ref[...] = back_half(error_ref, dec_ref, lax.axis_index("zh"))


def decoder_kernel(error_ref, feats_ref, grad_ref, bias_ref, done_ref, part_ref, sems):
    feats = feats_ref[...]
    copies = []
    for k in range(4):
        error = jnp.concatenate([error_ref[4 * k + j] for j in range(4)], axis=1)
        place = slice(k * WIDE, (k + 1) * WIDE)
        part_ref[k] = lax.dot_general(feats, error, TN, preferred_element_type=F32)
        copy = pltpu.make_async_copy(part_ref.at[k], grad_ref.at[:, place], sems.at[k])
        copy.start()
        copies.append(copy)
        bias_ref[:, place] = jnp.sum(error.astype(F32), axis=0, keepdims=True)
    done_ref[...] = jnp.zeros_like(done_ref)
    for copy in copies:
        copy.wait()


def pair_kernel(keep_ref, peer_ref, after_ref, out_ref):
    out_ref[...] = keep_ref[...] + peer_ref[...].astype(F32)


def encoder_kernel(own_ref, other_ref, pair_ref, near_ref, pos_ref, grad_ref, bias_ref):
    core, zh = lax.axis_index("core"), lax.axis_index("zh")
    quarter = FEATS // 4
    share = pair_ref[...] + near_ref[...]
    act = share * (2.0 * pos_ref[:, columns(zh, FEATS // 2)])
    act = jnp.where(core == 0, act[:, :quarter], act[:, quarter:])
    bias_ref[...] = jnp.sum(act, axis=0, keepdims=True)
    tiles = act.astype(BF16).astype(F32).reshape(COUNT // 8, 8, quarter)
    turned = pltpu.roll(tiles, 4, 1)
    sub = lax.broadcasted_iota(jnp.int32, tiles.shape, 1)
    zero = jnp.zeros_like(tiles)
    low = jnp.stack([jnp.where(sub < 4, tiles, zero), jnp.where(sub < 4, turned, zero)], axis=1)
    high = jnp.stack([jnp.where(sub < 4, zero, turned), jnp.where(sub < 4, zero, tiles)], axis=1)
    for h, side in enumerate((low, high)):
        side = side.reshape(2 * COUNT, quarter).astype(BF16)
        for ref, owner in ((own_ref, core), (other_ref, 1 - core)):
            grad_ref[:, columns(2 * owner + h, WIDE)] = lax.dot_general(
                side, ref[...], TN, preferred_element_type=F32
            )


def ring(step):
    index = lambda z: (z % 4) * 2 + z // 4
    return [(index(z), index((z + step) % 8)) for z in range(8)]


def mirror(x, axes, size, key):
    return lax.ppermute(x, axes, [(i, i ^ key) for i in range(size)])


def plane_swap(x, wide, key):
    pairs = []
    for i in range(32):
        y, x_at, core = i // 8, i // 2 % 4, i % 2
        along_x = wide == (core == 0)
        there = (y, x_at ^ key) if along_x else (y ^ key, x_at)
        pairs.append((i, 8 * there[0] + 2 * there[1] + core))
    return lax.ppermute(x, ("y", "x", "core"), pairs)


def plane_groups():
    ids = np.arange(256).reshape(4, 4, 4, 2, 2)
    return [
        [int(ids[(z, c % 4, c // 4) if core == 0 else (z, c // 4, c % 4)][zh, core]) for c in range(J)]
        for z, zh, core in np.ndindex(4, 2, 2)
    ]


def body(tokens, encoder_weight, encoder_bias, decoder_weight, decoder_bias, targets):
    sds, vmem = jax.ShapeDtypeStruct, pltpu.VMEM
    dec = decoder_weight[0]

    far_rows, *near_rows = [lax.ppermute(tokens, ("zl", "zh"), ring(step)) for step in (2, 1, 7)]
    tokens, encoder_weight = call(
        load_kernel,
        (vmem(tokens.shape, BF16), vmem(encoder_weight.shape, BF16)),
        tokens, encoder_weight,
        in_specs=[pl.BlockSpec(memory_space=pl.ANY)] * 2,
        scratch_shapes=[pltpu.SemaphoreType.DMA((2,))],
    )
    packed = call(pack_kernel, vmem((J, 8 * ROWS, WIDE), BF16), tokens, far_rows, *near_rows, vmem=range(4))
    own = lax.all_to_all(packed, ("y", "x"), 0, 0, tiled=True)
    own = own.reshape(2 * COUNT, WIDE)
    other = mirror(own, "core", 2, 1)

    wide, piece = (COUNT, WIDE), (COUNT, PIECE)
    send2, positive, feats = call(
        forward_kernel,
        (vmem(wide, BF16), vmem((COUNT, FEATS), F32), vmem((COUNT, FEATS), BF16)),
        own, other, encoder_weight, encoder_bias[None], dec, targets[0],
        vmem=(0, 1, 2, 4, 5),
        scratch_shapes=[vmem(wide, F32)],
    )
    moved2 = plane_swap(send2, True, 2)
    keep, send1, send3 = call(
        rest_kernel,
        (vmem(wide, F32), vmem(wide, BF16), vmem(wide, BF16)),
        feats, dec, targets[0],
        vmem=range(3),
        scratch_shapes=[vmem((2,) + wide, F32)],
    )
    moved = [plane_swap(send1, True, 1), moved2, plane_swap(send3, True, 3)]
    keep, *sends = call(middle_kernel, (vmem(piece, F32),) + (vmem(piece, BF16),) * 3, keep, *moved, vmem=range(4))
    moved = [plane_swap(sends[key - 1], False, key) for key in (2, 1, 3)]
    part = call(sum_kernel, vmem(piece, BF16), keep, *moved, vmem=range(4))
    moved = [mirror(part, "zl", DEPTH, key) for key in (2, 3, 1)]
    copies = call(error_kernel, vmem((J,) + piece, BF16), part, *moved, decoder_bias, vmem=range(4))
    errors = lax.all_to_all(copies, FEAT + TGT, 0, 0, axis_index_groups=plane_groups(), tiled=True)

    half = (COUNT, FEATS // 2)
    send = call(send_kernel, vmem(half, BF16), errors, dec, vmem=range(2))
    peer = mirror(send, "zh", 2, 1)
    keep = call(keep_kernel, vmem(half, F32), errors, dec, vmem=range(2))
    decoder_grad, bias_grad, done = call(
        decoder_kernel,
        (sds((FEATS, D), F32), sds((1, D), F32), vmem((8, 128), F32)),
        errors, feats,
        vmem=range(2),
        out_specs=(
            pl.BlockSpec(memory_space=pl.ANY),
            pl.BlockSpec(memory_space=pltpu.VMEM),
            pl.BlockSpec(memory_space=pltpu.VMEM),
        ),
        scratch_shapes=[vmem((4, FEATS, WIDE), F32), pltpu.SemaphoreType.DMA((4,))],
    )
    pair = call(pair_kernel, vmem(half, F32), keep, peer, done, vmem=range(3))
    near = mirror(pair, "core", 2, 1)
    encoder_grad, encoder_bias_grad = call(
        encoder_kernel,
        (sds((FEATS // 4, D), F32), sds((1, FEATS // 4), F32)),
        own, other, pair, near, positive,
        vmem=range(5),
    )
    return encoder_grad.T, encoder_bias_grad[0], decoder_grad[None], bias_grad


def solution(mesh):
    split = Mesh(mesh.devices.reshape(4, 4, 4, 2, 2), FEAT + TGT)
    return jax.shard_map(
        body,
        mesh=split,
        in_specs=(
            P(FEAT, None),
            P(None, FEAT),
            P(FEAT),
            P(TGT, FEAT, None),
            P(TGT, None),
            P(TGT, FEAT, None),
        ),
        out_specs=(
            P(None, FEAT + TGT),
            P(FEAT + TGT),
            P(TGT, FEAT, None),
            P(TGT, None),
        ),
        check_vma=False,
    )
```
